32 devices in a mesh: groups: 2 (over x), tm: 8 (over z, y), chan: 2 (over core).
Axes of the slice: x: 2, y: 2, z: 4, core: 2. Of those that a mesh axis runs over, the one named last changes fastest.
Arguments:
- record: bfloat16 [4096, 1024], P(('groups', 'tm'), 'chan'), parts along dimension 0, may hold values from -6 to 6
- pca_map: bfloat16 [1024, 128], P('chan'), may hold values from -0.1875 to 0.1875
- offsets: int32 [16], P(('groups', 'tm')), parts along dimension 0, may hold values from -192 to 192
- exclusion: int32 [2], P('groups'), parts along dimension 0, may hold values from 32 to 128
Outputs:
- profile: float32 [4096], P(('groups', 'tm')), parts along dimension 0
The draws below stay inside these ranges and needn't reach their ends.
There are 2 independent parts, one for each index of `groups`. The reference program is written for one: setup_inputs(seed, part) draws one part's arguments, and reference() takes and returns one part's arrays. A program takes and returns all parts, laid end to end along the dimension named above; an argument that names none is the same for every part. Nothing has to cross between parts.
All inputs are finite; a program needn't handle non-finite values.
Results may differ from the reference program's by a relative error of at most 0.0018.
Values may be sent and summed in bfloat16 or wider, within the bound.
No kernel may reach another device: no remote copies, remote signals or barrier semaphores. Data moves between devices by JAX's collectives and lax.ppermute only.
A program may use at most 128 MiB of HBM per device.

```python
import jax
import jax.numpy as jnp
from jax import lax

CH = 1024
DP = 128
M = 256
L = 256
SLABS = 8
TT = 2048
W = 64
N_TM = 8


def set_ends(array, own_key, least, largest):
    longest = array.shape.index(max(array.shape))
    spots = []
    for shift in (0, 1):
        where = [jax.random.randint(jax.random.fold_in(own_key, axis), (), 0, length) for axis, length in enumerate(array.shape)]
        where[longest] = (where[longest] + shift) % array.shape[longest]
        spots.append(tuple(where))
    return array.at[spots[0]].set(least).at[spots[1]].set(largest)


def level_of(own_key, extent, split, smallest, largest):
    level = 1.0
    for position, blocks in split:
        steps = jax.random.uniform(jax.random.fold_in(jax.random.fold_in(own_key, 6), position), (blocks,), jnp.float32, smallest / len(split), largest / len(split))
        level = level * jnp.repeat(jnp.exp(steps), extent[position] // blocks).reshape((-1,) + (1,) * (len(extent) - 1 - position))
    return level


def scatter_about(own_key, shape, scale, reach, cuts=(), kind=jnp.bfloat16):
    gain = level_of(own_key, shape, cuts, -0.22, 0.18) if cuts else 1.0
    drawn = jax.random.normal(own_key, shape, jnp.float32) * scale * gain
    return jnp.minimum(jnp.maximum(drawn, -reach), reach).astype(kind)


def setup_inputs(seed: int = 0, part: int = 0) -> dict:
    key_list = jax.random.split(jax.random.key(seed), 5)
    own_keys = jax.random.split(jax.random.fold_in(key_list[4], part), 5)
    record = scatter_about(own_keys[0], (TT, CH), 1.0, 6.0, ((0, 8), (1, 2)))
    pca_map = scatter_about(key_list[1], (CH, DP), CH ** -0.5, 0.1875, ((0, 2),))
    offsets = set_ends(jax.random.randint(own_keys[2], (SLABS,), L // 4 - L, L - L // 4 + 1), jax.random.fold_in(own_keys[2], 1), L // 4 - L, (L - L // 4 + 1) - 1).astype(jnp.int32)
    exclusion = jax.random.randint(own_keys[3], (1,), L // 8, L // 2 + 1).astype(jnp.int32)
    return {"record": record, "pca_map": pca_map, "offsets": offsets, "exclusion": exclusion}


def normalize(segment, rows):
    index = jnp.arange(rows)[:, None] + jnp.arange(M)[None, :]
    hankel = segment.astype(jnp.float32)[index]
    center = lax.optimization_barrier(jnp.mean(hankel, axis=1, keepdims=True))
    spread = lax.optimization_barrier(jnp.mean(hankel * hankel, axis=1, keepdims=True)) - center * center
    scale = jnp.sqrt(spread + 1e-05) * float(M * DP) ** 0.25
    normed = ((hankel - center) / scale).astype(jnp.bfloat16)
    return normed.reshape(rows, M * hankel.shape[2])

def reference(record, pca_map, offsets, exclusion):
    proj = jnp.dot(record, pca_map, preferred_element_type=jnp.float32).astype(jnp.bfloat16)
    looped = jnp.concatenate([proj, proj[:M - 1]], axis=0)

    def slab_windows(slab):
        first = (slab % N_TM * L).astype(jnp.int32)
        segment = lax.dynamic_slice_in_dim(looped, first, L + M - 1, 0)
        return normalize(segment, L)
    within = jnp.arange(L).astype(jnp.int32)
    diff = within[None, :] - within[:, None]

    def one_slab(slab):
        query = slab_windows(slab)
        near = jnp.dot(query, slab_windows(slab + 1).T, preferred_element_type=jnp.float32)
        far = jnp.dot(query, slab_windows(slab + N_TM // 2).T, preferred_element_type=jnp.float32)
        centre = offsets[slab]
        keep = (diff >= centre - W) & (diff <= centre + W) & (L + diff >= exclusion[0])
        near = jnp.where(keep, near, jnp.float32(-1e+30))
        rows_best = jnp.maximum(lax.optimization_barrier(jnp.max(near, axis=1)), lax.optimization_barrier(jnp.max(far, axis=1)))
        return (rows_best, lax.optimization_barrier(jnp.max(near, axis=0)))
    rows_best, cols_best = lax.map(one_slab, jnp.arange(N_TM).astype(jnp.int32))
    cols_best = jnp.roll(cols_best, 1, axis=0)
    return jnp.maximum(rows_best, cols_best).reshape(TT)
```

```python
import jax
import jax.numpy as jnp
from jax import lax
from jax.experimental import pallas as pl
from jax.experimental.pallas import tpu as pltpu
from jax.sharding import PartitionSpec as P

M = 256
SHIFTS = 16
GROUP = 4
NEG = -1e30


def window_stats(values, rows, scale):
    span = values.shape[0]
    row_pos = lax.broadcasted_iota(jnp.int32, (rows, span), 0)
    col_pos = lax.broadcasted_iota(jnp.int32, (rows, span), 1)
    inside = (col_pos >= row_pos) & (col_pos < row_pos + M)
    band = jnp.where(inside, 1.0, 0.0).astype(jnp.bfloat16)
    square = values * values
    upper = square.astype(jnp.bfloat16)
    lower = (square - upper.astype(jnp.float32)).astype(jnp.bfloat16)
    sums = jnp.dot(band, values.astype(jnp.bfloat16), preferred_element_type=jnp.float32)
    squares = jnp.dot(band, upper, preferred_element_type=jnp.float32)
    squares += jnp.dot(band, lower, preferred_element_type=jnp.float32)
    center = sums / M
    spread = squares / M - center * center
    return center, 1.0 / (jnp.sqrt(spread + 1e-05) * scale)


def tile_kernel(limits, q_head, q_tail, k_head, k_tail, best, wide, shifted, center, inverse, total):
    rows, depth = q_head.shape
    reach = shifted.shape[2]
    scale = float(M * depth) ** 0.25
    for side, (head, tail) in enumerate(((q_head, q_tail), (k_head, k_tail))):
        wide[0:rows, :] = head[...].astype(jnp.float32)
        wide[rows : rows + M, :] = tail[...].astype(jnp.float32)
        center[side], inverse[side] = window_stats(wide[...], rows, scale)
        for shift in range(SHIFTS):
            shifted[side, shift] = wide[shift : shift + reach, :].astype(jnp.bfloat16)
    total[...] = jnp.zeros_like(total)

    def normed(side, shift, base):
        window = shifted[side, shift, pl.ds(base, rows), :].astype(jnp.float32)
        return ((window - center[side]) * inverse[side]).astype(jnp.bfloat16)

    def step(index, carry):
        base = pl.multiple_of(index * SHIFTS, SHIFTS)
        added = jnp.zeros_like(total)
        for first in range(0, SHIFTS, GROUP):
            shifts = range(first, first + GROUP)
            left = jnp.concatenate([normed(0, shift, base) for shift in shifts], axis=1)
            right = jnp.concatenate([normed(1, shift, base) for shift in shifts], axis=1)
            added += lax.dot_general(
                left, right, (((1,), (1,)), ((), ())), preferred_element_type=jnp.float32
            )
        total[...] += added
        return carry

    lax.fori_loop(0, M // SHIFTS, step, 0)
    row_pos = lax.broadcasted_iota(jnp.int32, (rows, rows), 0)
    col_pos = lax.broadcasted_iota(jnp.int32, (rows, rows), 1)
    diff = col_pos - row_pos
    keep = (diff >= limits[0]) & (diff <= limits[1]) & (rows + diff >= limits[2])
    score = jnp.where(keep, total[...], NEG)
    row_best = jnp.max(score, axis=1, keepdims=True)
    best[0:1, :] = jnp.max(jnp.where(diff == 0, row_best, NEG), axis=0, keepdims=True)
    best[1:2, :] = jnp.max(score, axis=0, keepdims=True)


def tile_best(limits, q_head, q_tail, k_head, k_tail):
    rows, depth = q_head.shape
    vmem = pl.BlockSpec(memory_space=pltpu.VMEM)
    reach = rows + M - SHIFTS
    return pl.pallas_call(
        tile_kernel,
        out_shape=jax.ShapeDtypeStruct((2, rows), jnp.float32),
        in_specs=[pl.BlockSpec(memory_space=pltpu.SMEM), vmem, vmem, vmem, vmem],
        out_specs=vmem,
        scratch_shapes=[
            pltpu.VMEM((rows + M, depth), jnp.float32),
            pltpu.VMEM((2, SHIFTS, reach, depth), jnp.bfloat16),
            pltpu.VMEM((2, rows, depth), jnp.float32),
            pltpu.VMEM((2, rows, depth), jnp.float32),
            pltpu.VMEM((rows, rows), jnp.float32),
        ],
        compiler_params=pltpu.CompilerParams(vmem_limit_bytes=32 << 20),
        name="tile_best",
    )(limits, q_head, q_tail, k_head, k_tail)


def fetched(value, near_steps, far_steps):
    cycle = lax.axis_size("tm")
    pairs = []
    for slab in range(cycle):
        for core, steps in ((0, near_steps), (1, far_steps)):
            pairs.append(((slab + steps) % cycle * 2 + core, slab * 2 + core))
    return lax.ppermute(value, ("tm", "chan"), pairs)


def swapped(value):
    return lax.ppermute(value, "chan", [(0, 1), (1, 0)])


def per_device(record, pca_map, offsets, exclusion):
    core = lax.axis_index("chan")
    cycle = lax.axis_size("tm")
    rows = record.shape[0]
    quarter = rows // 4
    partial_value = jnp.dot(record, pca_map, preferred_element_type=jnp.float32)
    proj = (partial_value + swapped(partial_value)).astype(jnp.bfloat16)
    k_head = fetched(proj, 1, cycle // 2)
    k_tail = fetched(proj, 2, cycle // 2 + 1)
    q_tail = jnp.where(core == 0, k_head, swapped(k_head))
    centre = offsets[0]
    near = jnp.stack([centre - quarter, centre + quarter, exclusion[0]])
    far = jnp.array([-2 * rows, 2 * rows, -2 * rows], jnp.int32)
    best = tile_best(jnp.where(core == 0, near, far), proj, q_tail, k_head, k_tail)
    row_best = best[0]
    col_best = jnp.where(core == 0, best[1], NEG)
    col_back = lax.ppermute(col_best, "tm", [(slab, (slab + 1) % cycle) for slab in range(cycle)])
    own = jnp.maximum(row_best, col_back)
    return jnp.maximum(own, swapped(own))


def solution(mesh):
    in_specs = (P(("groups", "tm"), "chan"), P("chan", None), P(("groups", "tm")), P("groups"))
    out_specs = P(("groups", "tm"))
    return jax.shard_map(
        per_device, mesh=mesh, in_specs=in_specs, out_specs=out_specs, check_vma=False
    )
```

```python
import jax
import jax.numpy as jnp
from jax import lax
from jax.experimental import pallas as pl
from jax.experimental.pallas import tpu as pltpu
from jax.sharding import PartitionSpec as P

M = 256
SHIFTS = 64
BLOCK = 64
NEG = -1e30
UNITS = 2


def in_unit(body, shape, units):
    pl.run_scoped(body, *[pltpu.ACC(unit)(shape, jnp.float32) for unit in units])


def window_stats(sides, wide, center, inverse):
    rows, depth = sides[0][0].shape
    scale = float(M * depth) ** 0.25
    row_pos = lax.broadcasted_iota(jnp.int32, (rows, rows), 0)
    col_pos = lax.broadcasted_iota(jnp.int32, (rows, rows), 1)
    upper = jnp.where(col_pos >= row_pos, 1.0, 0.0).astype(jnp.bfloat16)
    lower = jnp.where(col_pos < row_pos, 1.0, 0.0).astype(jnp.bfloat16)

    def scoped(*totals):
        rest = []
        for side, parts in enumerate(sides):
            for half, band in enumerate((upper, lower)):
                value = parts[half][...]
                exact = value.astype(jnp.float32)
                wide[side, half * rows : (half + 1) * rows, :] = exact
                square = exact * exact
                rounded = square.astype(jnp.bfloat16)
                rest.append((square - rounded.astype(jnp.float32)).astype(jnp.bfloat16))
                both = jnp.concatenate([value, rounded], axis=1)
                pltpu.matmul_push_rhs(both, staging_register=half, mxu_index=side)
                pltpu.matmul_acc_lhs(totals[side], band, load_staged_rhs=half)
        for half, band in enumerate((upper, lower)):
            both = jnp.concatenate([rest[half], rest[2 + half]], axis=1)
            pltpu.matmul_push_rhs(both, staging_register=half, mxu_index=half)
            pltpu.matmul_acc_lhs(totals[2 + half], band, load_staged_rhs=half)
        small = pltpu.matmul_pop(totals[2]) + pltpu.matmul_pop(totals[3])
        for side in range(2):
            sums = pltpu.matmul_pop(totals[side])
            squares = sums[:, depth:] + small[:, side * depth : (side + 1) * depth]
            mean = sums[:, :depth] / M
            spread = squares / M - mean * mean
            center[side] = mean
            inverse[side] = (1.0 / (jnp.sqrt(spread + 1e-05) * scale))

    in_unit(scoped, (rows, 2 * depth), (0, 1, 0, 1))


def tile_kernel(limits, q_head, q_tail, k_head, k_tail, best, wide, center, inverse):
    rows, depth = q_head.shape
    blocks = rows // BLOCK
    window_stats(((q_head, q_tail), (k_head, k_tail)), wide, center, inverse)

    def normed(side, base, shift, first, count):
        here = slice(first, first + count)
        mean, scale = center[side, here], inverse[side, here]
        parts = []
        for step in range(shift, shift + 2 * UNITS):
            window = wide[side, pl.ds(base + first + step, count), :]
            parts.append(((window - mean) * scale).astype(jnp.bfloat16))
        return [jnp.concatenate(parts[2 * unit : 2 * unit + 2], axis=1) for unit in range(UNITS)]

    def scoped(*totals):
        def step(index, carry):
            base = pl.multiple_of(index * SHIFTS, SHIFTS)
            for shift in range(0, SHIFTS, 2 * UNITS):
                staging = shift // (2 * UNITS) % 2
                keys = normed(1, base, shift, 0, rows)
                for unit in range(UNITS):
                    pltpu.matmul_push_rhs(
                        keys[unit], staging_register=staging, mxu_index=unit, transpose=True
                    )
                for block in range(blocks):
                    query = normed(0, base, shift, block * BLOCK, BLOCK)
                    for unit in range(UNITS):
                        pltpu.matmul_acc_lhs(
                            totals[unit * blocks + block],
                            query[unit],
                            load_staged_rhs=staging if block == 0 else None,
                        )
            return carry

        lax.fori_loop(0, M // SHIFTS, step, 0)
        col_best = None
        for block in range(blocks):
            first = block * BLOCK
            row_pos = first + lax.broadcasted_iota(jnp.int32, (BLOCK, rows), 0)
            col_pos = lax.broadcasted_iota(jnp.int32, (BLOCK, rows), 1)
            diff = col_pos - row_pos
            keep = (diff >= limits[0]) & (diff <= limits[1]) & (rows + diff >= limits[2])
            total = pltpu.matmul_pop(totals[block]) + pltpu.matmul_pop(totals[blocks + block])
            score = jnp.where(keep, total, NEG)
            row_best = jnp.where(diff == 0, jnp.max(score, axis=1, keepdims=True), NEG)
            both = [jnp.max(value, axis=0, keepdims=True) for value in (row_best, score)]
            col_best = both if block == 0 else [jnp.maximum(*two) for two in zip(col_best, both)]
        best[0:1, :], best[1:2, :] = col_best

    in_unit(scoped, (BLOCK, rows), [unit for unit in range(UNITS) for _ in range(blocks)])


def tile_best(limits, q_head, q_tail, k_head, k_tail):
    rows, depth = q_head.shape
    vmem = pl.BlockSpec(memory_space=pltpu.VMEM)
    return pl.pallas_call(
        tile_kernel,
        out_shape=jax.ShapeDtypeStruct((2, rows), jnp.float32),
        in_specs=[pl.BlockSpec(memory_space=pltpu.SMEM), vmem, vmem, vmem, vmem],
        out_specs=vmem,
        scratch_shapes=[
            pltpu.VMEM((2, rows + M, depth), jnp.float32),
            pltpu.VMEM((2, rows, depth), jnp.float32),
            pltpu.VMEM((2, rows, depth), jnp.float32),
        ],
        compiler_params=pltpu.CompilerParams(vmem_limit_bytes=16 << 20),
        name="tile_best",
    )(limits, q_head, q_tail, k_head, k_tail)


def fetched(value, near_steps, far_steps):
    cycle = lax.axis_size("tm")
    pairs = []
    for slab in range(cycle):
        for core, steps in ((0, near_steps), (1, far_steps)):
            if steps is not None:
                pairs.append(((slab + steps) % cycle * 2 + core, slab * 2 + core))
    return lax.ppermute(value, ("tm", "chan"), pairs)


def swapped(value):
    return lax.ppermute(value, "chan", [(0, 1), (1, 0)])


def per_device(record, pca_map, offsets, exclusion):
    core = lax.axis_index("chan")
    cycle = lax.axis_size("tm")
    rows = record.shape[0]
    quarter = rows // 4
    partial_value = jnp.dot(record, pca_map, preferred_element_type=jnp.float32)
    proj = (partial_value + swapped(partial_value)).astype(jnp.bfloat16)
    k_head = fetched(proj, 1, cycle // 2)
    k_tail = fetched(proj, 2, cycle // 2 + 1)
    k_head, k_tail = lax.optimization_barrier((k_head, k_tail))
    q_tail = jnp.where(core == 0, k_head, swapped(k_head))
    centre = offsets[0]
    near = jnp.stack([centre - quarter, centre + quarter, exclusion[0]])
    far = jnp.array([-2 * rows, 2 * rows, -2 * rows], jnp.int32)
    best = tile_best(jnp.where(core == 0, near, far), proj, q_tail, k_head, k_tail)
    row_best = best[0]
    col_best = jnp.where(core == 0, best[1], NEG)
    col_back = lax.ppermute(col_best, "tm", [(slab, (slab + 1) % cycle) for slab in range(cycle)])
    own = jnp.maximum(row_best, col_back)
    return jnp.maximum(own, swapped(own))


def solution(mesh):
    in_specs = (P(("groups", "tm"), "chan"), P("chan", None), P(("groups", "tm")), P("groups"))
    out_specs = P(("groups", "tm"))
    return jax.shard_map(
        per_device, mesh=mesh, in_specs=in_specs, out_specs=out_specs, check_vma=False
    )
```

```python
import jax
import jax.numpy as jnp
from jax import lax
from jax.experimental import pallas as pl
from jax.experimental.pallas import tpu as pltpu
from jax.sharding import PartitionSpec as P

M = 256
SHIFTS = 64
BLOCK = 64
NEG = -1e30
UNITS = 2


def in_unit(body, shape, units):
    pl.run_scoped(body, *[pltpu.ACC(unit)(shape, jnp.float32) for unit in units])


def window_stats(sides, wide, center, inverse):
    rows, depth = sides[1][0].shape
    scale = float(M * depth) ** 0.25
    row_pos = lax.broadcasted_iota(jnp.int32, (rows, rows), 0)
    col_pos = lax.broadcasted_iota(jnp.int32, (rows, rows), 1)
    upper = jnp.where(col_pos >= row_pos, 1.0, 0.0).astype(jnp.bfloat16)
    lower = jnp.where(col_pos < row_pos, 1.0, 0.0).astype(jnp.bfloat16)

    def scoped(*totals):
        rest = []
        for side, parts in enumerate(sides):
            for half, band in enumerate((upper, lower)):
                value = parts[half][0:rows, :]
                exact = value.astype(jnp.float32)
                wide[side, half * rows : (half + 1) * rows, :] = exact
                square = exact * exact
                rounded = square.astype(jnp.bfloat16)
                rest.append((square - rounded.astype(jnp.float32)).astype(jnp.bfloat16))
                both = jnp.concatenate([value, rounded], axis=1)
                pltpu.matmul_push_rhs(both, staging_register=half, mxu_index=side)
                pltpu.matmul_acc_lhs(totals[side], band, load_staged_rhs=half)
        for half, band in enumerate((upper, lower)):
            both = jnp.concatenate([rest[half], rest[2 + half]], axis=1)
            pltpu.matmul_push_rhs(both, staging_register=half, mxu_index=half)
            pltpu.matmul_acc_lhs(totals[2 + half], band, load_staged_rhs=half)
        small = pltpu.matmul_pop(totals[2]) + pltpu.matmul_pop(totals[3])
        for side in range(2):
            sums = pltpu.matmul_pop(totals[side])
            squares = sums[:, depth:] + small[:, side * depth : (side + 1) * depth]
            mean = sums[:, :depth] / M
            spread = squares / M - mean * mean
            center[side] = mean
            inverse[side] = (1.0 / (jnp.sqrt(spread + 1e-05) * scale))

    in_unit(scoped, (rows, 2 * depth), (0, 1, 0, 1))


def tile_kernel(bounds, r_head, r_tail, c_head, c_tail, best, wide, center, inverse):
    rows, depth = c_head.shape
    blocks = rows // BLOCK
    window_stats(((r_head, r_tail), (c_head, c_tail)), wide, center, inverse)

    def normed(side, base, shift, first, count):
        here = slice(first, first + count)
        mean, scale = center[side, here], inverse[side, here]
        parts = []
        for step in range(shift, shift + 2 * UNITS):
            window = wide[side, pl.ds(base + first + step, count), :]
            parts.append(((window - mean) * scale).astype(jnp.bfloat16))
        return [jnp.concatenate(parts[2 * unit : 2 * unit + 2], axis=1) for unit in range(UNITS)]

    def scoped(*totals):
        def step(index, carry):
            base = pl.multiple_of(index * SHIFTS, SHIFTS)
            for shift in range(0, SHIFTS, 2 * UNITS):
                staging = shift // (2 * UNITS) % 2
                keys = normed(1, base, shift, 0, rows)
                for unit in range(UNITS):
                    pltpu.matmul_push_rhs(
                        keys[unit], staging_register=staging, mxu_index=unit, transpose=True
                    )
                for block in range(blocks):
                    query = normed(0, base, shift, block * BLOCK, BLOCK)
                    for unit in range(UNITS):
                        pltpu.matmul_acc_lhs(
                            totals[unit * blocks + block],
                            query[unit],
                            load_staged_rhs=staging if block == 0 else None,
                        )
            return carry

        lax.fori_loop(0, M // SHIFTS, step, 0)
        quarter = rows // 4
        centre = r_head[rows : rows + 1, 0:1].astype(jnp.float32).astype(jnp.int32)
        found = None
        for block in range(blocks):
            row_pos = block * BLOCK + lax.broadcasted_iota(jnp.int32, (BLOCK, rows), 0)
            col_pos = lax.broadcasted_iota(jnp.int32, (BLOCK, rows), 1)
            diff = col_pos - row_pos
            away = jnp.abs(diff - centre)
            keep = (away <= quarter + bounds[0]) & (rows + diff >= bounds[1])
            total = pltpu.matmul_pop(totals[block]) + pltpu.matmul_pop(totals[blocks + block])
            score = jnp.where(keep, total, NEG)
            row_best = jnp.where(diff == 0, jnp.max(score, axis=1, keepdims=True), NEG)
            both = [jnp.max(value, axis=0, keepdims=True) for value in (score, row_best)]
            found = both if found is None else [jnp.maximum(*two) for two in zip(found, both)]
        best[0:1, :], best[1:2, :] = found

    in_unit(scoped, (BLOCK, rows), [unit for unit in range(UNITS) for _ in range(blocks)])


def tile_best(bounds, r_head, r_tail, c_head, c_tail):
    rows, depth = c_head.shape
    vmem = pl.BlockSpec(memory_space=pltpu.VMEM)
    return pl.pallas_call(
        tile_kernel,
        out_shape=jax.ShapeDtypeStruct((2, rows), jnp.float32),
        in_specs=[pl.BlockSpec(memory_space=pltpu.SMEM), vmem, vmem, vmem, vmem],
        out_specs=vmem,
        scratch_shapes=[
            pltpu.VMEM((2, rows + M, depth), jnp.float32),
            pltpu.VMEM((2, rows, depth), jnp.float32),
            pltpu.VMEM((2, rows, depth), jnp.float32),
        ],
        compiler_params=pltpu.CompilerParams(vmem_limit_bytes=16 << 20),
        name="tile_best",
    )(bounds, r_head, r_tail, c_head, c_tail)


def fetched(value, near_steps, far_steps):
    cycle = lax.axis_size("tm")
    pairs = []
    for slab in range(cycle):
        for core, steps in ((0, near_steps), (1, far_steps)):
            if steps is not None:
                pairs.append(((slab + steps) % cycle * 2 + core, slab * 2 + core))
    return lax.ppermute(value, ("tm", "chan"), pairs)


def swapped(value):
    return lax.ppermute(value, "chan", [(0, 1), (1, 0)])


def per_device(record, pca_map, offsets, exclusion):
    core = lax.axis_index("chan")
    cycle = lax.axis_size("tm")
    rows = record.shape[0]
    partial_value = jnp.dot(record, pca_map, preferred_element_type=jnp.float32)
    proj = (partial_value + swapped(partial_value)).astype(jnp.bfloat16)
    note = jnp.broadcast_to(offsets.astype(jnp.bfloat16)[:, None], (16, proj.shape[1]))
    noted = jnp.concatenate([proj, note], axis=0)
    r_head = fetched(noted, -1, cycle // 2)
    second = fetched(proj, 1, cycle // 2 + 1)
    r_head, second = lax.optimization_barrier((r_head, second))
    r_tail = jnp.where(core == 0, proj, second)
    c_tail = jnp.where(core == 0, second, swapped(second))
    bounds = jnp.stack([core * 4 * rows, exclusion[0] - core * 4 * rows])
    best = tile_best(bounds, r_head, r_tail, proj, c_tail)
    row_back = lax.ppermute(best[1], "tm", [(slab, (slab - 1) % cycle) for slab in range(cycle)])
    own = jnp.where(core == 0, jnp.maximum(best[0], row_back), best[0])
    return jnp.maximum(own, swapped(own))


def solution(mesh):
    in_specs = (P(("groups", "tm"), "chan"), P("chan", None), P(("groups", "tm")), P("groups"))
    out_specs = P(("groups", "tm"))
    return jax.shard_map(
        per_device, mesh=mesh, in_specs=in_specs, out_specs=out_specs, check_vma=False
    )
```

```python
import functools

import jax
import jax.numpy as jnp
from jax import lax
from jax.experimental import pallas as pl
from jax.experimental.pallas import tpu as pltpu
from jax.sharding import PartitionSpec as P

M = 256
SHIFTS = 64
BLOCK = 64
NEG = -1e30
UNITS = 2
CHUNKS = 1


def in_unit(body, shape, units):
    pl.run_scoped(body, *[pltpu.ACC(unit)(shape, jnp.float32) for unit in units])


def window_stats(sides, wide, center, inverse):
    rows, depth = sides[1][0].shape
    scale = float(M * depth) ** 0.25
    row_pos = lax.broadcasted_iota(jnp.int32, (rows, rows), 0)
    col_pos = lax.broadcasted_iota(jnp.int32, (rows, rows), 1)
    upper = jnp.where(col_pos >= row_pos, 1.0, 0.0).astype(jnp.bfloat16)
    lower = jnp.where(col_pos < row_pos, 1.0, 0.0).astype(jnp.bfloat16)

    def scoped(*totals):
        rest = []
        for side, parts in enumerate(sides):
            for half, band in enumerate((upper, lower)):
                value = parts[half][0:rows, :]
                exact = value.astype(jnp.float32)
                wide[side, half * rows : (half + 1) * rows, :] = exact
                square = exact * exact
                rounded = square.astype(jnp.bfloat16)
                rest.append((square - rounded.astype(jnp.float32)).astype(jnp.bfloat16))
                both = jnp.concatenate([value, rounded], axis=1)
                pltpu.matmul_push_rhs(both, staging_register=half, mxu_index=side)
                pltpu.matmul_acc_lhs(totals[side], band, load_staged_rhs=half)
        for half, band in enumerate((upper, lower)):
            both = jnp.concatenate([rest[half], rest[2 + half]], axis=1)
            pltpu.matmul_push_rhs(both, staging_register=half, mxu_index=half)
            pltpu.matmul_acc_lhs(totals[2 + half], band, load_staged_rhs=half)
        small = pltpu.matmul_pop(totals[2]) + pltpu.matmul_pop(totals[3])
        for side in range(2):
            sums = pltpu.matmul_pop(totals[side])
            squares = sums[:, depth:] + small[:, side * depth : (side + 1) * depth]
            mean = sums[:, :depth] / M
            spread = squares / M - mean * mean
            center[side] = mean
            inverse[side] = (1.0 / (jnp.sqrt(spread + 1e-05) * scale))

    in_unit(scoped, (rows, 2 * depth), (0, 1, 0, 1))


def tile_kernel(bounds, r_head, r_tail, c_head, c_tail, best, wide, center, inverse):
    rows, depth = c_head.shape
    blocks = rows // BLOCK
    window_stats(((r_head, r_tail), (c_head, c_tail)), wide, center, inverse)

    def normed(side, base, shift, first, count):
        here = slice(first, first + count)
        mean, scale = center[side, here], inverse[side, here]
        parts = []
        for step in range(shift, shift + 2 * UNITS):
            window = wide[side, pl.ds(base + first + step, count), :]
            parts.append(((window - mean) * scale).astype(jnp.bfloat16))
        return [jnp.concatenate(parts[2 * unit : 2 * unit + 2], axis=1) for unit in range(UNITS)]

    def scoped(*totals):
        def step(index, carry):
            base = pl.multiple_of(index * SHIFTS, SHIFTS)
            for shift in range(0, SHIFTS, 2 * UNITS):
                staging = shift // (2 * UNITS) % 2
                keys = normed(1, base, shift, 0, rows)
                for unit in range(UNITS):
                    pltpu.matmul_push_rhs(
                        keys[unit], staging_register=staging, mxu_index=unit, transpose=True
                    )
                for block in range(blocks):
                    query = normed(0, base, shift, block * BLOCK, BLOCK)
                    for unit in range(UNITS):
                        pltpu.matmul_acc_lhs(
                            totals[unit * blocks + block],
                            query[unit],
                            load_staged_rhs=staging if block == 0 else None,
                        )
            return carry

        lax.fori_loop(0, M // SHIFTS, step, 0)
        quarter = rows // 4
        centre = r_head[rows : rows + 1, 0:1].astype(jnp.float32).astype(jnp.int32)
        found = None
        for block in range(blocks):
            row_pos = block * BLOCK + lax.broadcasted_iota(jnp.int32, (BLOCK, rows), 0)
            col_pos = lax.broadcasted_iota(jnp.int32, (BLOCK, rows), 1)
            diff = col_pos - row_pos
            away = jnp.abs(diff - centre)
            keep = (away <= quarter + bounds[0]) & (rows + diff >= bounds[1])
            total = pltpu.matmul_pop(totals[block]) + pltpu.matmul_pop(totals[blocks + block])
            score = jnp.where(keep, total, NEG)
            row_best = jnp.where(diff == 0, jnp.max(score, axis=1, keepdims=True), NEG)
            both = [jnp.max(value, axis=0, keepdims=True) for value in (score, row_best)]
            found = both if found is None else [jnp.maximum(*two) for two in zip(found, both)]
        best[0:1, :], best[1:2, :] = found

    in_unit(scoped, (BLOCK, rows), [unit for unit in range(UNITS) for _ in range(blocks)])


def tile_best(bounds, r_head, r_tail, c_head, c_tail):
    rows, depth = c_head.shape
    vmem = pl.BlockSpec(memory_space=pltpu.VMEM)
    return pl.pallas_call(
        tile_kernel,
        out_shape=jax.ShapeDtypeStruct((2, rows), jnp.float32),
        in_specs=[pl.BlockSpec(memory_space=pltpu.SMEM), vmem, vmem, vmem, vmem],
        out_specs=vmem,
        scratch_shapes=[
            pltpu.VMEM((2, rows + M, depth), jnp.float32),
            pltpu.VMEM((2, rows, depth), jnp.float32),
            pltpu.VMEM((2, rows, depth), jnp.float32),
        ],
        compiler_params=pltpu.CompilerParams(vmem_limit_bytes=16 << 20),
        name="tile_best",
    )(bounds, r_head, r_tail, c_head, c_tail)


def project_kernel(chunk, record, pca_map, partial_sum, samples, weights, arrived):
    copies = [pltpu.make_async_copy(pca_map, weights, arrived.at[0])]
    for first in range(0, record.shape[0], chunk):
        here = pl.ds(first, chunk)
        sem = arrived.at[1 + first // chunk]
        copies.append(pltpu.make_async_copy(record.at[here], samples.at[here], sem))
    for copy in copies:
        copy.start()
    copies[0].wait()
    for first, copy in zip(range(0, record.shape[0], chunk), copies[1:]):
        copy.wait()
        here = slice(first, first + chunk)
        partial_sum[here, :] = jnp.dot(
            samples[here, :], weights[...], preferred_element_type=jnp.float32
        )


def project(record, pca_map):
    rows, depth = record.shape[0], pca_map.shape[1]
    chunk = rows // CHUNKS
    hbm = pl.BlockSpec(memory_space=pltpu.HBM)
    return pl.pallas_call(
        functools.partial(project_kernel, chunk),
        out_shape=pltpu.VMEM((rows, depth), jnp.float32),
        in_specs=[hbm, hbm],
        out_specs=pl.BlockSpec(memory_space=pltpu.VMEM),
        scratch_shapes=[
            pltpu.VMEM(record.shape, record.dtype),
            pltpu.VMEM(pca_map.shape, pca_map.dtype),
            pltpu.SemaphoreType.DMA((1 + CHUNKS,)),
        ],
        compiler_params=pltpu.CompilerParams(vmem_limit_bytes=4 << 20),
        name="project",
    )(*(pltpu.with_memory_space_constraint(x, pltpu.HBM) for x in (record, pca_map)))


def fetched(value, near_steps, far_steps):
    cycle = lax.axis_size("tm")
    pairs = []
    for slab in range(cycle):
        for core, steps in ((0, near_steps), (1, far_steps)):
            if steps is not None:
                pairs.append(((slab + steps) % cycle * 2 + core, slab * 2 + core))
    return lax.ppermute(value, ("tm", "chan"), pairs)


def swapped(value):
    return lax.ppermute(value, "chan", [(0, 1), (1, 0)])


def per_device(record, pca_map, offsets, exclusion):
    core = lax.axis_index("chan")
    cycle = lax.axis_size("tm")
    rows = record.shape[0]
    partial_value = project(record, pca_map)
    proj = (partial_value + swapped(partial_value)).astype(jnp.bfloat16)
    note = jnp.broadcast_to(offsets.astype(jnp.bfloat16)[:, None], (16, proj.shape[1]))
    noted = jnp.concatenate([proj, note], axis=0)
    r_head = fetched(noted, -1, cycle // 2)
    second = fetched(proj, 1, cycle // 2 + 1)
    r_head, second = lax.optimization_barrier((r_head, second))
    r_tail = jnp.where(core == 0, proj, second)
    c_tail = jnp.where(core == 0, second, swapped(second))
    bounds = jnp.stack([core * 4 * rows, exclusion[0] - core * 4 * rows])
    best = tile_best(bounds, r_head, r_tail, proj, c_tail)
    row_back = lax.ppermute(best[1], "tm", [(slab, (slab - 1) % cycle) for slab in range(cycle)])
    own = jnp.where(core == 0, jnp.maximum(best[0], row_back), best[0])
    return jnp.maximum(own, swapped(own))


def solution(mesh):
    in_specs = (P(("groups", "tm"), "chan"), P("chan", None), P(("groups", "tm")), P("groups"))
    out_specs = P(("groups", "tm"))
    return jax.shard_map(
        per_device, mesh=mesh, in_specs=in_specs, out_specs=out_specs, check_vma=False
    )
```

```python
import functools

import jax
import jax.numpy as jnp
from jax import lax
from jax.experimental import pallas as pl
from jax.experimental.pallas import tpu as pltpu
from jax.sharding import PartitionSpec as P

M = 256
SHIFTS = 64
BLOCK = 64
NEG = -1e30
UNITS = 2
CHUNKS = 1


def in_unit(body, shape, units):
    pl.run_scoped(body, *[pltpu.ACC(unit)(shape, jnp.float32) for unit in units])


def window_stats(sides, wide, center, inverse):
    rows, depth = sides[1][0].shape
    scale = float(M * depth) ** 0.25
    row_pos = lax.broadcasted_iota(jnp.int32, (rows, rows), 0)
    col_pos = lax.broadcasted_iota(jnp.int32, (rows, rows), 1)
    upper = jnp.where(col_pos >= row_pos, 1.0, 0.0).astype(jnp.bfloat16)
    lower = jnp.where(col_pos < row_pos, 1.0, 0.0).astype(jnp.bfloat16)

    def scoped(*totals):
        rest = []
        for side, parts in enumerate(sides):
            for half, band in enumerate((upper, lower)):
                value = parts[half][0:rows, :]
                exact = value.astype(jnp.float32)
                wide[side, half * rows : (half + 1) * rows, :] = exact
                square = exact * exact
                rounded = square.astype(jnp.bfloat16)
                rest.append((square - rounded.astype(jnp.float32)).astype(jnp.bfloat16))
                both = jnp.concatenate([value, rounded], axis=1)
                pltpu.matmul_push_rhs(both, staging_register=half, mxu_index=side)
                pltpu.matmul_acc_lhs(totals[side], band, load_staged_rhs=half)
        for half, band in enumerate((upper, lower)):
            both = jnp.concatenate([rest[half], rest[2 + half]], axis=1)
            pltpu.matmul_push_rhs(both, staging_register=half, mxu_index=half)
            pltpu.matmul_acc_lhs(totals[2 + half], band, load_staged_rhs=half)
        small = pltpu.matmul_pop(totals[2]) + pltpu.matmul_pop(totals[3])
        for side in range(2):
            sums = pltpu.matmul_pop(totals[side])
            squares = sums[:, depth:] + small[:, side * depth : (side + 1) * depth]
            mean = sums[:, :depth] / M
            spread = squares / M - mean * mean
            center[side] = mean
            inverse[side] = (1.0 / (jnp.sqrt(spread + 1e-05) * scale))

    in_unit(scoped, (rows, 2 * depth), (0, 1, 0, 1))


def tile_kernel(zone, r_head, r_tail, c_head, c_tail, best, wide, center, inverse):
    rows, depth = c_head.shape
    blocks = rows // BLOCK
    window_stats(((r_head, r_tail), (c_head, c_tail)), wide, center, inverse)

    def normed(side, base, shift, first, count):
        here = slice(first, first + count)
        mean, scale = center[side, here], inverse[side, here]
        parts = []
        for step in range(shift, shift + 2 * UNITS):
            window = wide[side, pl.ds(base + first + step, count), :]
            parts.append(((window - mean) * scale).astype(jnp.bfloat16))
        return [jnp.concatenate(parts[2 * unit : 2 * unit + 2], axis=1) for unit in range(UNITS)]

    def scoped(*totals):
        def step(index, carry):
            base = pl.multiple_of(index * SHIFTS, SHIFTS)
            for shift in range(0, SHIFTS, 2 * UNITS):
                staging = shift // (2 * UNITS) % 2
                keys = normed(1, base, shift, 0, rows)
                for unit in range(UNITS):
                    pltpu.matmul_push_rhs(
                        keys[unit], staging_register=staging, mxu_index=unit, transpose=True
                    )
                for block in range(blocks):
                    query = normed(0, base, shift, block * BLOCK, BLOCK)
                    for unit in range(UNITS):
                        pltpu.matmul_acc_lhs(
                            totals[unit * blocks + block],
                            query[unit],
                            load_staged_rhs=staging if block == 0 else None,
                        )
            return carry

        lax.fori_loop(0, M // SHIFTS, step, 0)
        quarter = rows // 4
        note = r_head[rows : rows + 16, :].astype(jnp.float32).astype(jnp.int32)
        centre, excluded = note[0:1, 0:1], zone[0:1, 0:1]
        free = lax.axis_index("chan") * 4 * rows
        found = None
        for block in range(blocks):
            row_pos = block * BLOCK + lax.broadcasted_iota(jnp.int32, (BLOCK, rows), 0)
            col_pos = lax.broadcasted_iota(jnp.int32, (BLOCK, rows), 1)
            diff = col_pos - row_pos
            away = jnp.abs(diff - centre)
            keep = (away <= quarter + free) & (rows + diff + free >= excluded)
            total = pltpu.matmul_pop(totals[block]) + pltpu.matmul_pop(totals[blocks + block])
            score = jnp.where(keep, total, NEG)
            row_best = jnp.where(diff == 0, jnp.max(score, axis=1, keepdims=True), NEG)
            both = [jnp.max(value, axis=0, keepdims=True) for value in (score, row_best)]
            found = both if found is None else [jnp.maximum(*two) for two in zip(found, both)]
        best[0:1, :], best[1:2, :] = found

    in_unit(scoped, (BLOCK, rows), [unit for unit in range(UNITS) for _ in range(blocks)])


def tile_best(zone, r_head, r_tail, c_head, c_tail):
    rows, depth = c_head.shape
    vmem = pl.BlockSpec(memory_space=pltpu.VMEM)
    return pl.pallas_call(
        tile_kernel,
        out_shape=jax.ShapeDtypeStruct((2, rows), jnp.float32),
        in_specs=[vmem, vmem, vmem, vmem, vmem],
        out_specs=vmem,
        scratch_shapes=[
            pltpu.VMEM((2, rows + M, depth), jnp.float32),
            pltpu.VMEM((2, rows, depth), jnp.float32),
            pltpu.VMEM((2, rows, depth), jnp.float32),
        ],
        compiler_params=pltpu.CompilerParams(vmem_limit_bytes=16 << 20),
        name="tile_best",
    )(zone, r_head, r_tail, c_head, c_tail)


def project_kernel(chunk, record, pca_map, partial_sum, samples, weights, arrived):
    copies = [pltpu.make_async_copy(pca_map, weights, arrived.at[0])]
    for first in range(0, record.shape[0], chunk):
        here = pl.ds(first, chunk)
        sem = arrived.at[1 + first // chunk]
        copies.append(pltpu.make_async_copy(record.at[here], samples.at[here], sem))
    for copy in copies:
        copy.start()
    copies[0].wait()
    for first, copy in zip(range(0, record.shape[0], chunk), copies[1:]):
        copy.wait()
        here = slice(first, first + chunk)
        partial_sum[here, :] = jnp.dot(
            samples[here, :], weights[...], preferred_element_type=jnp.float32
        )


def project(record, pca_map):
    rows, depth = record.shape[0], pca_map.shape[1]
    chunk = rows // CHUNKS
    hbm = pl.BlockSpec(memory_space=pltpu.HBM)
    return pl.pallas_call(
        functools.partial(project_kernel, chunk),
        out_shape=pltpu.VMEM((rows, depth), jnp.float32),
        in_specs=[hbm, hbm],
        out_specs=pl.BlockSpec(memory_space=pltpu.VMEM),
        scratch_shapes=[
            pltpu.VMEM(record.shape, record.dtype),
            pltpu.VMEM(pca_map.shape, pca_map.dtype),
            pltpu.SemaphoreType.DMA((1 + CHUNKS,)),
        ],
        compiler_params=pltpu.CompilerParams(vmem_limit_bytes=4 << 20),
        name="project",
    )(*(pltpu.with_memory_space_constraint(x, pltpu.HBM) for x in (record, pca_map)))


def fetched(value, near_steps, far_steps):
    cycle = lax.axis_size("tm")
    pairs = []
    for slab in range(cycle):
        for core, steps in ((0, near_steps), (1, far_steps)):
            if steps is not None:
                pairs.append(((slab + steps) % cycle * 2 + core, slab * 2 + core))
    return lax.ppermute(value, ("tm", "chan"), pairs)


def swapped(value):
    return lax.ppermute(value, "chan", [(0, 1), (1, 0)])


def per_device(record, pca_map, offsets, exclusion):
    core = lax.axis_index("chan")
    cycle = lax.axis_size("tm")
    rows = record.shape[0]
    partial_value = project(record, pca_map)
    proj = (partial_value + swapped(partial_value)).astype(jnp.bfloat16)
    note = jnp.broadcast_to(offsets.astype(jnp.bfloat16)[:, None], (16, proj.shape[1]))
    noted = jnp.concatenate([proj, note], axis=0)
    r_head = fetched(noted, -1, cycle // 2)
    second = fetched(proj, 1, cycle // 2 + 1)
    r_head, second = lax.optimization_barrier((r_head, second))
    r_tail = jnp.where(core == 0, proj, second)
    c_tail = jnp.where(core == 0, second, swapped(second))
    zone = jnp.broadcast_to(exclusion[:, None], (8, proj.shape[1]))
    best = tile_best(zone, r_head, r_tail, proj, c_tail)
    row_back = lax.ppermute(best[1], "tm", [(slab, (slab - 1) % cycle) for slab in range(cycle)])
    own = jnp.where(core == 0, jnp.maximum(best[0], row_back), best[0])
    return jnp.maximum(own, swapped(own))


def solution(mesh):
    in_specs = (P(("groups", "tm"), "chan"), P("chan", None), P(("groups", "tm")), P("groups"))
    out_specs = P(("groups", "tm"))
    return jax.shard_map(
        per_device, mesh=mesh, in_specs=in_specs, out_specs=out_specs, check_vma=False
    )
```

```python
import functools

import jax
import jax.numpy as jnp
from jax import lax
from jax.experimental import pallas as pl
from jax.experimental.pallas import tpu as pltpu
from jax.sharding import PartitionSpec as P

M = 256
SHIFTS = 64
BLOCK = 64
NEG = -1e30
UNITS = 2
CHUNKS = 1


def in_unit(body, shape, units):
    pl.run_scoped(body, *[pltpu.ACC(unit)(shape, jnp.float32) for unit in units])


def window_stats(sides, wide, center, inverse):
    rows, depth = sides[1][0].shape
    scale = float(M * depth) ** 0.25
    row_pos = lax.broadcasted_iota(jnp.int32, (rows, rows), 0)
    col_pos = lax.broadcasted_iota(jnp.int32, (rows, rows), 1)
    upper = jnp.where(col_pos >= row_pos, 1.0, 0.0).astype(jnp.bfloat16)
    lower = jnp.where(col_pos < row_pos, 1.0, 0.0).astype(jnp.bfloat16)

    def scoped(*totals):
        rest = []
        for side, parts in enumerate(sides):
            for half, band in enumerate((upper, lower)):
                value = parts[half][0:rows, :]
                exact = value.astype(jnp.float32)
                wide[side, half * rows : (half + 1) * rows, :] = exact
                square = exact * exact
                rounded = square.astype(jnp.bfloat16)
                rest.append((square - rounded.astype(jnp.float32)).astype(jnp.bfloat16))
                both = jnp.concatenate([value, rounded], axis=1)
                pltpu.matmul_push_rhs(both, staging_register=half, mxu_index=side)
                pltpu.matmul_acc_lhs(totals[side], band, load_staged_rhs=half)
        for half, band in enumerate((upper, lower)):
            both = jnp.concatenate([rest[half], rest[2 + half]], axis=1)
            pltpu.matmul_push_rhs(both, staging_register=half, mxu_index=half)
            pltpu.matmul_acc_lhs(totals[2 + half], band, load_staged_rhs=half)
        small = pltpu.matmul_pop(totals[2]) + pltpu.matmul_pop(totals[3])
        for side in range(2):
            sums = pltpu.matmul_pop(totals[side])
            squares = sums[:, depth:] + small[:, side * depth : (side + 1) * depth]
            mean = sums[:, :depth] / M
            spread = squares / M - mean * mean
            center[side] = mean
            inverse[side] = (1.0 / (jnp.sqrt(spread + 1e-05) * scale))

    in_unit(scoped, (rows, 2 * depth), (0, 1, 0, 1))


def tile_kernel(zone, r_head, r_tail, c_head, c_tail, best, wide, center, inverse):
    rows, depth = c_head.shape
    blocks = rows // BLOCK
    window_stats(((r_head, r_tail), (c_head, c_tail)), wide, center, inverse)

    def normed(side, base, shift, first, count):
        here = slice(first, first + count)
        mean, scale = center[side, here], inverse[side, here]
        parts = []
        for step in range(shift, shift + 2 * UNITS):
            window = wide[side, pl.ds(base + first + step, count), :]
            parts.append(((window - mean) * scale).astype(jnp.bfloat16))
        return [jnp.concatenate(parts[2 * unit : 2 * unit + 2], axis=1) for unit in range(UNITS)]

    def scoped(*totals):
        def step(index, carry):
            base = pl.multiple_of(index * SHIFTS, SHIFTS)
            for shift in range(0, SHIFTS, 2 * UNITS):
                staging = shift // (2 * UNITS) % 2
                keys = normed(1, base, shift, 0, rows)
                for unit in range(UNITS):
                    pltpu.matmul_push_rhs(
                        keys[unit], staging_register=staging, mxu_index=unit, transpose=True
                    )
                for block in range(blocks):
                    query = normed(0, base, shift, block * BLOCK, BLOCK)
                    for unit in range(UNITS):
                        pltpu.matmul_acc_lhs(
                            totals[unit * blocks + block],
                            query[unit],
                            load_staged_rhs=staging if block == 0 else None,
                        )
            return carry

        lax.fori_loop(0, M // SHIFTS, step, 0)
        quarter = rows // 4
        note = r_head[rows : rows + 16, :].astype(jnp.float32).astype(jnp.int32)
        centre, excluded = note[0:1, 0:1], zone[0:1, 0:1]
        free = lax.axis_index("chan") * 4 * rows
        found = None
        for block in range(blocks):
            row_pos = block * BLOCK + lax.broadcasted_iota(jnp.int32, (BLOCK, rows), 0)
            col_pos = lax.broadcasted_iota(jnp.int32, (BLOCK, rows), 1)
            diff = col_pos - row_pos
            away = jnp.abs(diff - centre)
            keep = (away <= quarter + free) & (rows + diff + free >= excluded)
            total = pltpu.matmul_pop(totals[block]) + pltpu.matmul_pop(totals[blocks + block])
            score = jnp.where(keep, total, NEG)
            row_best = jnp.where(diff == 0, jnp.max(score, axis=1, keepdims=True), NEG)
            both = [jnp.max(value, axis=0, keepdims=True) for value in (score, row_best)]
            found = both if found is None else [jnp.maximum(*two) for two in zip(found, both)]
        best[0:1, :], best[1:2, :] = found

    in_unit(scoped, (BLOCK, rows), [unit for unit in range(UNITS) for _ in range(blocks)])


def tile_best(zone, r_head, r_tail, c_head, c_tail):
    rows, depth = c_head.shape
    vmem = pl.BlockSpec(memory_space=pltpu.VMEM)
    return pl.pallas_call(
        tile_kernel,
        out_shape=jax.ShapeDtypeStruct((2, rows), jnp.float32),
        in_specs=[vmem, vmem, vmem, vmem, vmem],
        out_specs=vmem,
        scratch_shapes=[
            pltpu.VMEM((2, rows + M, depth), jnp.float32),
            pltpu.VMEM((2, rows, depth), jnp.float32),
            pltpu.VMEM((2, rows, depth), jnp.float32),
        ],
        compiler_params=pltpu.CompilerParams(vmem_limit_bytes=16 << 20),
        name="tile_best",
    )(zone, r_head, r_tail, c_head, c_tail)


def project_kernel(chunk, record, pca_map, partial_sum, samples, weights, arrived):
    copies = [pltpu.make_async_copy(pca_map, weights, arrived.at[0])]
    for first in range(0, record.shape[0], chunk):
        here = pl.ds(first, chunk)
        sem = arrived.at[1 + first // chunk]
        copies.append(pltpu.make_async_copy(record.at[here], samples.at[here], sem))
    for copy in copies:
        copy.start()
    copies[0].wait()
    for first, copy in zip(range(0, record.shape[0], chunk), copies[1:]):
        copy.wait()
        here = slice(first, first + chunk)
        partial_sum[here, :] = jnp.dot(
            samples[here, :], weights[...], preferred_element_type=jnp.float32
        )


def project(record, pca_map):
    rows, depth = record.shape[0], pca_map.shape[1]
    chunk = rows // CHUNKS
    hbm = pl.BlockSpec(memory_space=pltpu.HBM)
    return pl.pallas_call(
        functools.partial(project_kernel, chunk),
        out_shape=pltpu.VMEM((rows, depth), jnp.float32),
        in_specs=[hbm, hbm],
        out_specs=pl.BlockSpec(memory_space=pltpu.VMEM),
        scratch_shapes=[
            pltpu.VMEM(record.shape, record.dtype),
            pltpu.VMEM(pca_map.shape, pca_map.dtype),
            pltpu.SemaphoreType.DMA((1 + CHUNKS,)),
        ],
        compiler_params=pltpu.CompilerParams(vmem_limit_bytes=4 << 20),
        name="project",
    )(*(pltpu.with_memory_space_constraint(x, pltpu.HBM) for x in (record, pca_map)))


def fetched(value, near, far):
    pairs = []
    for slab in range(lax.axis_size("tm")):
        pairs += [(near[slab] * 2, slab * 2), (far[slab] * 2 + 1, slab * 2 + 1)]
    return lax.ppermute(value, ("tm", "chan"), pairs)


def swapped(value):
    return lax.ppermute(value, "chan", [(0, 1), (1, 0)])


def per_device(record, pca_map, offsets, exclusion):
    core = lax.axis_index("chan")
    cycle = lax.axis_size("tm")
    rows = record.shape[0]
    partial_value = project(record, pca_map)
    proj = (partial_value + swapped(partial_value)).astype(jnp.bfloat16)
    note = jnp.broadcast_to(offsets.astype(jnp.bfloat16)[:, None], (16, proj.shape[1]))
    noted = jnp.concatenate([proj, note], axis=0)
    half = cycle // 2
    turns = range(cycle)
    beside = [turn ^ 1 for turn in turns]
    r_head = fetched(noted, [(turn - 1) % cycle for turn in turns], [(turn + half) % cycle for turn in turns])
    second = fetched(proj, [(turn + 1) % cycle for turn in turns], [(turn + half + 1) % cycle for turn in turns])
    third = fetched(proj, beside, [(turn + 1) % cycle for turn in turns])
    r_head, second, third = lax.optimization_barrier((r_head, second, third))
    r_tail = jnp.where(core == 0, proj, second)
    c_tail = jnp.where(core == 0, second, third)
    zone = jnp.broadcast_to(exclusion[:, None], (8, proj.shape[1]))
    best = tile_best(zone, r_head, r_tail, proj, c_tail)
    row_back = fetched(best[1], [(turn + 1) % cycle for turn in turns], beside)
    own = jnp.where(core == 0, jnp.maximum(best[0], row_back), best[0])
    return jnp.maximum(own, swapped(own))


def solution(mesh):
    in_specs = (P(("groups", "tm"), "chan"), P("chan", None), P(("groups", "tm")), P("groups"))
    out_specs = P(("groups", "tm"))
    return jax.shard_map(
        per_device, mesh=mesh, in_specs=in_specs, out_specs=out_specs, check_vma=False
    )
```

```python
import functools

import jax
import jax.numpy as jnp
from jax import lax
from jax.experimental import pallas as pl
from jax.experimental.pallas import tpu as pltpu
from jax.sharding import PartitionSpec as P

M = 256
SHIFTS = 64
BLOCK = 64
NEG = -1e30
UNITS = 2
CHUNKS = 1


def in_unit(body, shape, units):
    pl.run_scoped(body, *[pltpu.ACC(unit)(shape, jnp.float32) for unit in units])


def window_stats(sides, wide, center, inverse):
    rows, depth = sides[0][1].shape
    scale = float(M * depth) ** 0.25
    row_pos = lax.broadcasted_iota(jnp.int32, (rows, rows), 0)
    col_pos = lax.broadcasted_iota(jnp.int32, (rows, rows), 1)
    upper = jnp.where(col_pos >= row_pos, 1.0, 0.0).astype(jnp.bfloat16)
    lower = jnp.where(col_pos < row_pos, 1.0, 0.0).astype(jnp.bfloat16)

    def scoped(*totals):
        rest = []
        for side, parts in enumerate(sides):
            for half, band in enumerate((upper, lower)):
                value = parts[half][0:rows, :]
                exact = value.astype(jnp.float32)
                wide[side, half * rows : (half + 1) * rows, :] = exact
                square = exact * exact
                rounded = square.astype(jnp.bfloat16)
                rest.append((square - rounded.astype(jnp.float32)).astype(jnp.bfloat16))
                both = jnp.concatenate([value, rounded], axis=1)
                pltpu.matmul_push_rhs(both, staging_register=half, mxu_index=side)
                pltpu.matmul_acc_lhs(totals[side], band, load_staged_rhs=half)
        for half, band in enumerate((upper, lower)):
            both = jnp.concatenate([rest[half], rest[2 + half]], axis=1)
            pltpu.matmul_push_rhs(both, staging_register=half, mxu_index=half)
            pltpu.matmul_acc_lhs(totals[2 + half], band, load_staged_rhs=half)
        small = pltpu.matmul_pop(totals[2]) + pltpu.matmul_pop(totals[3])
        for side in range(2):
            sums = pltpu.matmul_pop(totals[side])
            squares = sums[:, depth:] + small[:, side * depth : (side + 1) * depth]
            mean = sums[:, :depth] / M
            spread = squares / M - mean * mean
            center[side] = mean
            inverse[side] = (1.0 / (jnp.sqrt(spread + 1e-05) * scale))

    in_unit(scoped, (rows, 2 * depth), (0, 1, 0, 1))


def tile_kernel(zone, r_head, r_tail, c_head, c_tail, best, wide, center, inverse):
    rows, depth = r_tail.shape
    blocks = rows // BLOCK
    window_stats(((r_head, r_tail), (c_head, c_tail)), wide, center, inverse)

    def normed(side, base, shift, first, count):
        here = slice(first, first + count)
        mean, scale = center[side, here], inverse[side, here]
        parts = []
        for step in range(shift, shift + 2 * UNITS):
            window = wide[side, pl.ds(base + first + step, count), :]
            parts.append(((window - mean) * scale).astype(jnp.bfloat16))
        return [jnp.concatenate(parts[2 * unit : 2 * unit + 2], axis=1) for unit in range(UNITS)]

    def scoped(*totals):
        def step(index, carry):
            base = pl.multiple_of(index * SHIFTS, SHIFTS)
            for shift in range(0, SHIFTS, 2 * UNITS):
                staging = shift // (2 * UNITS) % 2
                keys = normed(1, base, shift, 0, rows)
                for unit in range(UNITS):
                    pltpu.matmul_push_rhs(
                        keys[unit], staging_register=staging, mxu_index=unit, transpose=True
                    )
                for block in range(blocks):
                    query = normed(0, base, shift, block * BLOCK, BLOCK)
                    for unit in range(UNITS):
                        pltpu.matmul_acc_lhs(
                            totals[unit * blocks + block],
                            query[unit],
                            load_staged_rhs=staging if block == 0 else None,
                        )
            return carry

        lax.fori_loop(0, M // SHIFTS, step, 0)
        quarter = rows // 4
        core = lax.axis_index("chan")
        edge = core * (lax.axis_index("tm") == lax.axis_size("tm") - 1).astype(jnp.int32)
        notes = [head[rows : rows + 16, :].astype(jnp.float32)[0:1, 0:1] for head in (r_head, c_head)]
        centre = jnp.where(core == 0, *notes).astype(jnp.int32)
        excluded = zone[0:1, 0:1]
        free = (core - edge) * 4 * rows
        found = None
        for block in range(blocks):
            row_pos = block * BLOCK + lax.broadcasted_iota(jnp.int32, (BLOCK, rows), 0)
            col_pos = lax.broadcasted_iota(jnp.int32, (BLOCK, rows), 1)
            diff = col_pos - row_pos
            ahead = diff * (1 - 2 * edge)
            away = jnp.abs(ahead - centre)
            keep = (away <= quarter + free) & (rows + ahead + free >= excluded)
            total = pltpu.matmul_pop(totals[block]) + pltpu.matmul_pop(totals[blocks + block])
            score = jnp.where(keep, total, NEG)
            row_best = jnp.where(diff == 0, jnp.max(score, axis=1, keepdims=True), NEG)
            both = [jnp.max(value, axis=0, keepdims=True) for value in (score, row_best)]
            found = both if found is None else [jnp.maximum(*two) for two in zip(found, both)]
        best[0:1, :], best[1:2, :] = found

    in_unit(scoped, (BLOCK, rows), [unit for unit in range(UNITS) for _ in range(blocks)])


def tile_best(zone, r_head, r_tail, c_head, c_tail):
    rows, depth = r_tail.shape
    vmem = pl.BlockSpec(memory_space=pltpu.VMEM)
    return pl.pallas_call(
        tile_kernel,
        out_shape=jax.ShapeDtypeStruct((2, rows), jnp.float32),
        in_specs=[vmem, vmem, vmem, vmem, vmem],
        out_specs=vmem,
        scratch_shapes=[
            pltpu.VMEM((2, rows + M, depth), jnp.float32),
            pltpu.VMEM((2, rows, depth), jnp.float32),
            pltpu.VMEM((2, rows, depth), jnp.float32),
        ],
        compiler_params=pltpu.CompilerParams(vmem_limit_bytes=16 << 20),
        name="tile_best",
    )(zone, r_head, r_tail, c_head, c_tail)


def project_kernel(chunk, record, pca_map, partial_sum, samples, weights, arrived):
    copies = [pltpu.make_async_copy(pca_map, weights, arrived.at[0])]
    for first in range(0, record.shape[0], chunk):
        here = pl.ds(first, chunk)
        sem = arrived.at[1 + first // chunk]
        copies.append(pltpu.make_async_copy(record.at[here], samples.at[here], sem))
    for copy in copies:
        copy.start()
    copies[0].wait()
    for first, copy in zip(range(0, record.shape[0], chunk), copies[1:]):
        copy.wait()
        here = slice(first, first + chunk)
        partial_sum[here, :] = jnp.dot(
            samples[here, :], weights[...], preferred_element_type=jnp.float32
        )


def project(record, pca_map):
    rows, depth = record.shape[0], pca_map.shape[1]
    chunk = rows // CHUNKS
    hbm = pl.BlockSpec(memory_space=pltpu.HBM)
    return pl.pallas_call(
        functools.partial(project_kernel, chunk),
        out_shape=pltpu.VMEM((rows, depth), jnp.float32),
        in_specs=[hbm, hbm],
        out_specs=pl.BlockSpec(memory_space=pltpu.VMEM),
        scratch_shapes=[
            pltpu.VMEM(record.shape, record.dtype),
            pltpu.VMEM(pca_map.shape, pca_map.dtype),
            pltpu.SemaphoreType.DMA((1 + CHUNKS,)),
        ],
        compiler_params=pltpu.CompilerParams(vmem_limit_bytes=4 << 20),
        name="project",
    )(*(pltpu.with_memory_space_constraint(x, pltpu.HBM) for x in (record, pca_map)))


def fetched(value, sources):
    pairs = []
    for slab, both in enumerate(sources):
        pairs += [(2 * turn + core, 2 * slab + place) for place, (turn, core) in enumerate(both)]
    return lax.ppermute(value, ("tm", "chan"), pairs)


def swapped(value):
    return lax.ppermute(value, "chan", [(0, 1), (1, 0)])


def per_device(record, pca_map, offsets, exclusion):
    core = lax.axis_index("chan")
    cycle = lax.axis_size("tm")
    rows = record.shape[0]
    partial_value = project(record, pca_map)
    proj = (partial_value + swapped(partial_value)).astype(jnp.bfloat16)
    note = jnp.broadcast_to(offsets.astype(jnp.bfloat16)[:, None], (16, proj.shape[1]))
    noted = jnp.concatenate([proj, note], axis=0)
    half = cycle // 2
    turns = range(cycle)
    last = cycle - 1
    edge = (core == 1) & (lax.axis_index("tm") == last)
    first = [(((turn - 1) % cycle, 0), ((turn + half) % cycle, 1)) for turn in turns]
    second = [((turn + 1, 0), ((turn + half + 1) % cycle, 1)) for turn in turns[:-1]] + [((0, 0), (1, 0))]
    second[0] = ((half, 1), second[0][1])
    third = [((turn, 1), ((turn + 1) % cycle, 0)) for turn in turns]
    third[0], third[1] = ((1, 1), (1, 0)), ((0, 1), third[1][1])
    r_head, second, third = [fetched(noted, first), fetched(proj, second), fetched(proj, third)]
    r_head, second, third = lax.optimization_barrier((r_head, second, third))
    r_head = jnp.where(edge, jnp.concatenate([third, note], axis=0), r_head)
    r_tail = jnp.where(core == 0, proj, second)
    c_tail = jnp.where((core == 1) | (lax.axis_index("tm") == 0), third[:rows], second)
    zone = jnp.broadcast_to(exclusion[:, None], (8, proj.shape[1]))
    best = tile_best(zone, r_head, r_tail, noted, c_tail)
    beyond = [(turn - 1, 1) for turn in turns]
    beyond[0], beyond[half], beyond[last] = (0, 0), (last - 1, 1), (half - 1, 1)
    back = [((turn + 1, 0), beyond[turn]) for turn in turns[:-1]] + [((last, 1), beyond[last])]
    back = fetched(best[1], back)
    wanted = jnp.where(core == 0, lax.axis_index("tm") != last, edge)
    own = jnp.where(wanted, jnp.maximum(best[0], back), best[0])
    return jnp.maximum(own, swapped(own))


def solution(mesh):
    in_specs = (P(("groups", "tm"), "chan"), P("chan", None), P(("groups", "tm")), P("groups"))
    out_specs = P(("groups", "tm"))
    return jax.shard_map(
        per_device, mesh=mesh, in_specs=in_specs, out_specs=out_specs, check_vma=False
    )
```

```python
import functools

import jax
import jax.numpy as jnp
from jax import lax
from jax.experimental import pallas as pl
from jax.experimental.pallas import tpu as pltpu
from jax.sharding import PartitionSpec as P

M = 256
SHIFTS = 64
BLOCK = 64
NEG = -1e30
UNITS = 2
CHUNKS = 1


def in_unit(body, shape, units):
    pl.run_scoped(body, *[pltpu.ACC(unit)(shape, jnp.float32) for unit in units])


def window_stats(sides, wide, center, inverse):
    rows, depth = sides[0][1].shape
    scale = float(M * depth) ** 0.25
    row_pos = lax.broadcasted_iota(jnp.int32, (rows, rows), 0)
    col_pos = lax.broadcasted_iota(jnp.int32, (rows, rows), 1)
    upper = jnp.where(col_pos >= row_pos, 1.0, 0.0).astype(jnp.bfloat16)
    lower = jnp.where(col_pos < row_pos, 1.0, 0.0).astype(jnp.bfloat16)

    def scoped(*totals):
        rest = []
        for side, parts in enumerate(sides):
            for half, band in enumerate((upper, lower)):
                value = parts[half][0:rows, :]
                exact = value.astype(jnp.float32)
                wide[side, half * rows : (half + 1) * rows, :] = exact
                square = exact * exact
                rounded = square.astype(jnp.bfloat16)
                rest.append((square - rounded.astype(jnp.float32)).astype(jnp.bfloat16))
                both = jnp.concatenate([value, rounded], axis=1)
                pltpu.matmul_push_rhs(both, staging_register=half, mxu_index=side)
                pltpu.matmul_acc_lhs(totals[side], band, load_staged_rhs=half)
        for half, band in enumerate((upper, lower)):
            both = jnp.concatenate([rest[half], rest[2 + half]], axis=1)
            pltpu.matmul_push_rhs(both, staging_register=half, mxu_index=half)
            pltpu.matmul_acc_lhs(totals[2 + half], band, load_staged_rhs=half)
        small = pltpu.matmul_pop(totals[2]) + pltpu.matmul_pop(totals[3])
        for side in range(2):
            sums = pltpu.matmul_pop(totals[side])
            squares = sums[:, depth:] + small[:, side * depth : (side + 1) * depth]
            mean = sums[:, :depth] / M
            spread = squares / M - mean * mean
            center[side] = mean
            inverse[side] = (1.0 / (jnp.sqrt(spread + 1e-05) * scale))

    in_unit(scoped, (rows, 2 * depth), (0, 1, 0, 1))


def tile_kernel(zone, r_head, r_tail, c_head, c_tail, best, wide, center, inverse):
    rows, depth = r_tail.shape
    blocks = rows // BLOCK
    window_stats(((r_head, r_tail), (c_head, c_tail)), wide, center, inverse)

    def normed(side, base, shift, first, count):
        here = slice(first, first + count)
        mean, scale = center[side, here], inverse[side, here]
        parts = []
        for step in range(shift, shift + 2 * UNITS):
            window = wide[side, pl.ds(base + first + step, count), :]
            parts.append(((window - mean) * scale).astype(jnp.bfloat16))
        return [jnp.concatenate(parts[2 * unit : 2 * unit + 2], axis=1) for unit in range(UNITS)]

    def scoped(*totals):
        def step(index, carry):
            base = pl.multiple_of(index * SHIFTS, SHIFTS)
            for shift in range(0, SHIFTS, 2 * UNITS):
                staging = shift // (2 * UNITS) % 2
                keys = normed(1, base, shift, 0, rows)
                for unit in range(UNITS):
                    pltpu.matmul_push_rhs(
                        keys[unit], staging_register=staging, mxu_index=unit, transpose=True
                    )
                for block in range(blocks):
                    query = normed(0, base, shift, block * BLOCK, BLOCK)
                    for unit in range(UNITS):
                        pltpu.matmul_acc_lhs(
                            totals[unit * blocks + block],
                            query[unit],
                            load_staged_rhs=staging if block == 0 else None,
                        )
            return carry

        lax.fori_loop(0, M // SHIFTS, step, 0)
        quarter = rows // 4
        core = lax.axis_index("chan")
        edge = core * (lax.axis_index("tm") == lax.axis_size("tm") - 1).astype(jnp.int32)
        notes = [head[rows : rows + 16, :].astype(jnp.float32)[0:1, 0:1] for head in (r_head, c_head)]
        centre = jnp.where(core == 0, *notes).astype(jnp.int32)
        excluded = zone[0:1, 0:1]
        free = (core - edge) * 4 * rows
        found = None
        for block in range(blocks):
            row_pos = block * BLOCK + lax.broadcasted_iota(jnp.int32, (BLOCK, rows), 0)
            col_pos = lax.broadcasted_iota(jnp.int32, (BLOCK, rows), 1)
            diff = col_pos - row_pos
            ahead = diff * (1 - 2 * edge)
            away = jnp.abs(ahead - centre)
            keep = (away <= quarter + free) & (rows + ahead + free >= excluded)
            total = pltpu.matmul_pop(totals[block]) + pltpu.matmul_pop(totals[blocks + block])
            score = jnp.where(keep, total, NEG)
            row_best = jnp.where(diff == 0, jnp.max(score, axis=1, keepdims=True), NEG)
            both = [jnp.max(value, axis=0, keepdims=True) for value in (score, row_best)]
            found = both if found is None else [jnp.maximum(*two) for two in zip(found, both)]
        best[0:1, :], best[1:2, :] = found

    in_unit(scoped, (BLOCK, rows), [unit for unit in range(UNITS) for _ in range(blocks)])


def tile_best(zone, r_head, r_tail, c_head, c_tail):
    rows, depth = r_tail.shape
    vmem = pl.BlockSpec(memory_space=pltpu.VMEM)
    return pl.pallas_call(
        tile_kernel,
        out_shape=jax.ShapeDtypeStruct((2, rows), jnp.float32),
        in_specs=[vmem, vmem, vmem, vmem, vmem],
        out_specs=vmem,
        scratch_shapes=[
            pltpu.VMEM((2, rows + M, depth), jnp.float32),
            pltpu.VMEM((2, rows, depth), jnp.float32),
            pltpu.VMEM((2, rows, depth), jnp.float32),
        ],
        compiler_params=pltpu.CompilerParams(vmem_limit_bytes=16 << 20),
        name="tile_best",
    )(zone, r_head, r_tail, c_head, c_tail)


def project_kernel(chunk, record, pca_map, partial_sum, samples, weights, arrived):
    copies = [pltpu.make_async_copy(pca_map, weights, arrived.at[0])]
    for first in range(0, record.shape[0], chunk):
        here = pl.ds(first, chunk)
        sem = arrived.at[1 + first // chunk]
        copies.append(pltpu.make_async_copy(record.at[here], samples.at[here], sem))
    for copy in copies:
        copy.start()
    copies[0].wait()
    for first, copy in zip(range(0, record.shape[0], chunk), copies[1:]):
        copy.wait()
        here = slice(first, first + chunk)
        partial_sum[here, :] = jnp.dot(
            samples[here, :], weights[...], preferred_element_type=jnp.float32
        )


def project(record, pca_map):
    rows, depth = record.shape[0], pca_map.shape[1]
    chunk = rows // CHUNKS
    hbm = pl.BlockSpec(memory_space=pltpu.HBM)
    return pl.pallas_call(
        functools.partial(project_kernel, chunk),
        out_shape=pltpu.VMEM((rows, depth), jnp.float32),
        in_specs=[hbm, hbm],
        out_specs=pl.BlockSpec(memory_space=pltpu.VMEM),
        scratch_shapes=[
            pltpu.VMEM(record.shape, record.dtype),
            pltpu.VMEM(pca_map.shape, pca_map.dtype),
            pltpu.SemaphoreType.DMA((1 + CHUNKS,)),
        ],
        compiler_params=pltpu.CompilerParams(vmem_limit_bytes=4 << 20),
        name="project",
    )(*(pltpu.with_memory_space_constraint(x, pltpu.HBM) for x in (record, pca_map)))


def fetched(value, sources):
    pairs = []
    for slab, both in enumerate(sources):
        pairs += [(2 * turn + core, 2 * slab + place) for place, (turn, core) in enumerate(both)]
    return lax.ppermute(value, ("tm", "chan"), pairs)


def swapped(value):
    return lax.ppermute(value, "chan", [(0, 1), (1, 0)])


def per_device(record, pca_map, offsets, exclusion):
    core = lax.axis_index("chan")
    cycle = lax.axis_size("tm")
    rows = record.shape[0]
    partial_value = project(record, pca_map)
    proj = (partial_value + swapped(partial_value)).astype(jnp.bfloat16)
    note = jnp.broadcast_to(offsets.astype(jnp.bfloat16)[:, None], (16, proj.shape[1]))
    noted = jnp.concatenate([proj, note], axis=0)
    half = cycle // 2
    turns = range(cycle)
    last = cycle - 1
    edge = (core == 1) & (lax.axis_index("tm") == last)
    first = [(((turn - 1) % cycle, 0), ((turn + half) % cycle, 1)) for turn in turns]
    second = [((turn + 1, 0), ((turn + half + 1) % cycle, 1)) for turn in turns[:-1]] + [((half, 1), (0, 0))]
    third = [((turn, 1), (turn + 1, 0)) for turn in turns[:-1]] + [((0, 0), (1, 1))]
    for turn in range(1, last, 2):
        third[turn] = ((turn + 2, 1), third[turn][1])
    r_head, second, third = [fetched(noted, first), fetched(proj, second), fetched(proj, third)]
    r_head, second, third = lax.optimization_barrier((r_head, second, third))
    r_head = jnp.where(edge, jnp.concatenate([second, note], axis=0), r_head)
    r_tail = jnp.where(core == 0, proj, jnp.where(edge, third, second))
    c_tail = jnp.where((core == 1) ^ (lax.axis_index("tm") == last), third, second)
    zone = jnp.broadcast_to(exclusion[:, None], (8, proj.shape[1]))
    best = tile_best(zone, r_head, r_tail, noted, c_tail)
    beyond = [(turn - 1, 1) for turn in turns]
    beyond[0], beyond[half], beyond[last] = (0, 0), (last - 1, 1), (half - 1, 1)
    back = [((turn + 1, 0), beyond[turn]) for turn in turns[:-1]] + [((last, 1), beyond[last])]
    back = fetched(best[1], back)
    wanted = jnp.where(core == 0, lax.axis_index("tm") != last, edge)
    own = jnp.where(wanted, jnp.maximum(best[0], back), best[0])
    return jnp.maximum(own, swapped(own))


def solution(mesh):
    in_specs = (P(("groups", "tm"), "chan"), P("chan", None), P(("groups", "tm")), P("groups"))
    out_specs = P(("groups", "tm"))
    return jax.shard_map(
        per_device, mesh=mesh, in_specs=in_specs, out_specs=out_specs, check_vma=False
    )
```

```python
import functools

import jax
import jax.numpy as jnp
from jax import lax
from jax.experimental import pallas as pl
from jax.experimental.pallas import tpu as pltpu
from jax.sharding import PartitionSpec as P

M = 256
SHIFTS = 128
BLOCK = 64
NEG = -1e30
UNITS = 2
CHUNKS = 1


def in_unit(body, shape, units):
    pl.run_scoped(body, *[pltpu.ACC(unit)(shape, jnp.float32) for unit in units])


def window_stats(sides, wide, center, inverse):
    rows, depth = sides[0][1].shape
    scale = float(M * depth) ** 0.25
    row_pos = lax.broadcasted_iota(jnp.int32, (rows, rows), 0)
    col_pos = lax.broadcasted_iota(jnp.int32, (rows, rows), 1)
    upper = jnp.where(col_pos >= row_pos, 1.0, 0.0).astype(jnp.bfloat16)
    lower = jnp.where(col_pos < row_pos, 1.0, 0.0).astype(jnp.bfloat16)

    def scoped(*totals):
        rest = []
        for side, parts in enumerate(sides):
            for half, band in enumerate((upper, lower)):
                value = parts[half][0:rows, :]
                exact = value.astype(jnp.float32)
                wide[side, half * rows : (half + 1) * rows, :] = exact
                square = exact * exact
                rounded = square.astype(jnp.bfloat16)
                rest.append((square - rounded.astype(jnp.float32)).astype(jnp.bfloat16))
                both = jnp.concatenate([value, rounded], axis=1)
                pltpu.matmul_push_rhs(both, staging_register=half, mxu_index=side)
                pltpu.matmul_acc_lhs(totals[side], band, load_staged_rhs=half)
        for half, band in enumerate((upper, lower)):
            both = jnp.concatenate([rest[half], rest[2 + half]], axis=1)
            pltpu.matmul_push_rhs(both, staging_register=half, mxu_index=half)
            pltpu.matmul_acc_lhs(totals[2 + half], band, load_staged_rhs=half)
        small = pltpu.matmul_pop(totals[2]) + pltpu.matmul_pop(totals[3])
        for side in range(2):
            sums = pltpu.matmul_pop(totals[side])
            squares = sums[:, depth:] + small[:, side * depth : (side + 1) * depth]
            mean = sums[:, :depth] / M
            spread = squares / M - mean * mean
            center[side] = mean
            inverse[side] = (lax.rsqrt(spread + 1e-05) * (1.0 / scale))

    in_unit(scoped, (rows, 2 * depth), (0, 1, 0, 1))


def tile_kernel(zone, r_head, r_tail, c_head, c_tail, best, wide, center, inverse):
    rows, depth = r_tail.shape
    blocks = rows // BLOCK
    window_stats(((r_head, r_tail), (c_head, c_tail)), wide, center, inverse)

    def normed(side, base, shift, first, count):
        here = slice(first, first + count)
        mean, scale = center[side, here], inverse[side, here]
        parts = []
        for step in range(shift, shift + 2 * UNITS):
            window = wide[side, pl.ds(base + first + step, count), :]
            parts.append(((window - mean) * scale).astype(jnp.bfloat16))
        return [jnp.concatenate(parts[2 * unit : 2 * unit + 2], axis=1) for unit in range(UNITS)]

    def scoped(*totals):
        def step(index, carry):
            base = pl.multiple_of(index * SHIFTS, SHIFTS)
            for shift in range(0, SHIFTS, 2 * UNITS):
                staging = shift // (2 * UNITS) % 2
                keys = normed(1, base, shift, 0, rows)
                for unit in range(UNITS):
                    pltpu.matmul_push_rhs(
                        keys[unit], staging_register=staging, mxu_index=unit, transpose=True
                    )
                for block in range(blocks):
                    query = normed(0, base, shift, block * BLOCK, BLOCK)
                    for unit in range(UNITS):
                        pltpu.matmul_acc_lhs(
                            totals[unit * blocks + block],
                            query[unit],
                            load_staged_rhs=staging if block == 0 else None,
                        )
            return carry

        lax.fori_loop(0, M // SHIFTS, step, 0)
        quarter = rows // 4
        core = lax.axis_index("chan")
        edge = core * (lax.axis_index("tm") == lax.axis_size("tm") - 1).astype(jnp.int32)
        notes = [head[rows : rows + 16, :].astype(jnp.float32)[0:1, 0:1] for head in (r_head, c_head)]
        centre = jnp.where(core == 0, *notes).astype(jnp.int32)
        excluded = zone[0:1, 0:1]
        free = (core - edge) * 4 * rows
        found = None
        for block in range(blocks):
            row_pos = block * BLOCK + lax.broadcasted_iota(jnp.int32, (BLOCK, rows), 0)
            col_pos = lax.broadcasted_iota(jnp.int32, (BLOCK, rows), 1)
            diff = col_pos - row_pos
            ahead = diff * (1 - 2 * edge)
            away = jnp.abs(ahead - centre)
            keep = (away <= quarter + free) & (rows + ahead + free >= excluded)
            total = pltpu.matmul_pop(totals[block]) + pltpu.matmul_pop(totals[blocks + block])
            score = jnp.where(keep, total, NEG)
            row_best = jnp.where(diff == 0, jnp.max(score, axis=1, keepdims=True), NEG)
            both = [jnp.max(value, axis=0, keepdims=True) for value in (score, row_best)]
            found = both if found is None else [jnp.maximum(*two) for two in zip(found, both)]
        best[0:1, :], best[1:2, :] = found

    in_unit(scoped, (BLOCK, rows), [unit for unit in range(UNITS) for _ in range(blocks)])


def tile_best(zone, r_head, r_tail, c_head, c_tail):
    rows, depth = r_tail.shape
    vmem = pl.BlockSpec(memory_space=pltpu.VMEM)
    return pl.pallas_call(
        tile_kernel,
        out_shape=jax.ShapeDtypeStruct((2, rows), jnp.float32),
        in_specs=[vmem, vmem, vmem, vmem, vmem],
        out_specs=vmem,
        scratch_shapes=[
            pltpu.VMEM((2, rows + M, depth), jnp.float32),
            pltpu.VMEM((2, rows, depth), jnp.float32),
            pltpu.VMEM((2, rows, depth), jnp.float32),
        ],
        compiler_params=pltpu.CompilerParams(vmem_limit_bytes=16 << 20),
        name="tile_best",
    )(zone, r_head, r_tail, c_head, c_tail)


def project_kernel(chunk, record, pca_map, partial_sum, samples, weights, arrived):
    copies = [pltpu.make_async_copy(pca_map, weights, arrived.at[0])]
    for first in range(0, record.shape[0], chunk):
        here = pl.ds(first, chunk)
        sem = arrived.at[1 + first // chunk]
        copies.append(pltpu.make_async_copy(record.at[here], samples.at[here], sem))
    for copy in copies:
        copy.start()
    copies[0].wait()
    for first, copy in zip(range(0, record.shape[0], chunk), copies[1:]):
        copy.wait()
        here = slice(first, first + chunk)
        partial_sum[here, :] = jnp.dot(
            samples[here, :], weights[...], preferred_element_type=jnp.float32
        )


def project(record, pca_map):
    rows, depth = record.shape[0], pca_map.shape[1]
    chunk = rows // CHUNKS
    hbm = pl.BlockSpec(memory_space=pltpu.HBM)
    return pl.pallas_call(
        functools.partial(project_kernel, chunk),
        out_shape=pltpu.VMEM((rows, depth), jnp.float32),
        in_specs=[hbm, hbm],
        out_specs=pl.BlockSpec(memory_space=pltpu.VMEM),
        scratch_shapes=[
            pltpu.VMEM(record.shape, record.dtype),
            pltpu.VMEM(pca_map.shape, pca_map.dtype),
            pltpu.SemaphoreType.DMA((1 + CHUNKS,)),
        ],
        compiler_params=pltpu.CompilerParams(vmem_limit_bytes=4 << 20),
        name="project",
    )(*(pltpu.with_memory_space_constraint(x, pltpu.HBM) for x in (record, pca_map)))


def fetched(value, sources):
    pairs = []
    for slab, both in enumerate(sources):
        pairs += [(2 * turn + core, 2 * slab + place) for place, (turn, core) in enumerate(both)]
    return lax.ppermute(value, ("tm", "chan"), pairs)


def swapped(value):
    return lax.ppermute(value, "chan", [(0, 1), (1, 0)])


def per_device(record, pca_map, offsets, exclusion):
    core = lax.axis_index("chan")
    cycle = lax.axis_size("tm")
    rows = record.shape[0]
    partial_value = project(record, pca_map)
    proj = (partial_value + swapped(partial_value)).astype(jnp.bfloat16)
    note = jnp.broadcast_to(offsets.astype(jnp.bfloat16)[:, None], (16, proj.shape[1]))
    noted = jnp.concatenate([proj, note], axis=0)
    half = cycle // 2
    turns = range(cycle)
    last = cycle - 1
    edge = (core == 1) & (lax.axis_index("tm") == last)
    first = [(((turn - 1) % cycle, 0), ((turn + half) % cycle, 1)) for turn in turns]
    second = [(((turn + 1) % cycle, 0), ((turn + half + 1) % cycle, 1)) for turn in turns]
    second[half - 1], second[last] = ((half, 0), (half, 1)), ((0, 0), (0, 1))
    third = [((turn, 1), ((turn + 1) % cycle, 0)) for turn in turns]
    for turn in range(1, last, 2):
        third[turn] = ((turn + 2, 1), third[turn][1])
    third[half - 1], third[last] = (third[half - 1][0], (0, 0)), ((half, 0), (1, 1))
    r_head, second, third = [fetched(noted, first), fetched(proj, second), fetched(proj, third)]
    r_head, second, third = lax.optimization_barrier((r_head, second, third))
    r_head = jnp.where(edge, jnp.concatenate([second, note], axis=0), r_head)
    turned = (core == 1) & (lax.axis_index("tm") % half == half - 1)
    r_tail = jnp.where(core == 0, proj, jnp.where(turned, third, second))
    c_tail = jnp.where((core == 1) & ~turned, third, second)
    zone = jnp.broadcast_to(exclusion[:, None], (8, proj.shape[1]))
    best = tile_best(zone, r_head, r_tail, noted, c_tail)
    beyond = [(turn - 1, 1) for turn in turns]
    beyond[0], beyond[half], beyond[last] = (0, 0), (last - 1, 1), (half - 1, 1)
    back = [((turn + 1, 0), beyond[turn]) for turn in turns[:-1]] + [((last, 1), beyond[last])]
    back = fetched(best[1], back)
    wanted = jnp.where(core == 0, lax.axis_index("tm") != last, edge)
    own = jnp.where(wanted, jnp.maximum(best[0], back), best[0])
    return jnp.maximum(own, swapped(own))


def solution(mesh):
    in_specs = (P(("groups", "tm"), "chan"), P("chan", None), P(("groups", "tm")), P("groups"))
    out_specs = P(("groups", "tm"))
    return jax.shard_map(
        per_device, mesh=mesh, in_specs=in_specs, out_specs=out_specs, check_vma=False
    )
```

```python
import functools

import jax
import jax.numpy as jnp
from jax import lax
from jax.experimental import pallas as pl
from jax.experimental.pallas import tpu as pltpu
from jax.sharding import PartitionSpec as P

M = 256
SHIFTS = 128
BLOCK = 64
NEG = -1e30
UNITS = 2
CHUNKS = 1


def in_unit(body, shape, units):
    pl.run_scoped(body, *[pltpu.ACC(unit)(shape, jnp.float32) for unit in units])


def window_stats(sides, wide, center, inverse):
    rows, depth = sides[0][1].shape
    scale = float(M * depth) ** 0.25
    row_pos = lax.broadcasted_iota(jnp.int32, (rows, rows), 0)
    col_pos = lax.broadcasted_iota(jnp.int32, (rows, rows), 1)
    upper = jnp.where(col_pos >= row_pos, 1.0, 0.0).astype(jnp.bfloat16)
    lower = jnp.where(col_pos < row_pos, 1.0, 0.0).astype(jnp.bfloat16)

    def scoped(*totals):
        rest = []
        for side, parts in enumerate(sides):
            for half, band in enumerate((upper, lower)):
                value = parts[half][0:rows, :]
                exact = value.astype(jnp.float32)
                wide[side, half * rows : (half + 1) * rows, :] = exact
                square = exact * exact
                rounded = square.astype(jnp.bfloat16)
                rest.append((square - rounded.astype(jnp.float32)).astype(jnp.bfloat16))
                both = jnp.concatenate([value, rounded], axis=1)
                pltpu.matmul_push_rhs(both, staging_register=half, mxu_index=side)
                pltpu.matmul_acc_lhs(totals[side], band, load_staged_rhs=half)
        for half, band in enumerate((upper, lower)):
            both = jnp.concatenate([rest[half], rest[2 + half]], axis=1)
            pltpu.matmul_push_rhs(both, staging_register=half, mxu_index=half)
            pltpu.matmul_acc_lhs(totals[2 + half], band, load_staged_rhs=half)
        small = pltpu.matmul_pop(totals[2]) + pltpu.matmul_pop(totals[3])
        for side in range(2):
            sums = pltpu.matmul_pop(totals[side])
            squares = sums[:, depth:] + small[:, side * depth : (side + 1) * depth]
            mean = sums[:, :depth] / M
            spread = squares / M - mean * mean
            center[side] = mean
            inverse[side] = (lax.rsqrt(spread + 1e-05) * (1.0 / scale))

    in_unit(scoped, (rows, 2 * depth), (0, 1, 0, 1))


def tile_kernel(zone, r_head, r_tail, c_head, c_tail, best, wide, center, inverse):
    rows, depth = r_tail.shape
    blocks = rows // BLOCK
    window_stats(((r_head, r_tail), (c_head, c_tail)), wide, center, inverse)

    def normed(side, base, shift, first, count):
        here = slice(first, first + count)
        mean, scale = center[side, here], inverse[side, here]
        parts = []
        for step in range(shift, shift + 2 * UNITS):
            window = wide[side, pl.ds(base + first + step, count), :]
            parts.append(((window - mean) * scale).astype(jnp.bfloat16))
        return [jnp.concatenate(parts[2 * unit : 2 * unit + 2], axis=1) for unit in range(UNITS)]

    def scoped(*totals):
        def step(index, carry):
            base = pl.multiple_of(index * SHIFTS, SHIFTS)
            for shift in range(0, SHIFTS, 2 * UNITS):
                staging = shift // (2 * UNITS) % 2
                keys = normed(1, base, shift, 0, rows)
                for unit in range(UNITS):
                    pltpu.matmul_push_rhs(
                        keys[unit], staging_register=staging, mxu_index=unit, transpose=True
                    )
                for block in range(blocks):
                    query = normed(0, base, shift, block * BLOCK, BLOCK)
                    for unit in range(UNITS):
                        pltpu.matmul_acc_lhs(
                            totals[unit * blocks + block],
                            query[unit],
                            load_staged_rhs=staging if block == 0 else None,
                        )
            return carry

        lax.fori_loop(0, M // SHIFTS, step, 0)
        quarter = rows // 4
        core = lax.axis_index("chan")
        edge = core * (lax.axis_index("tm") == lax.axis_size("tm") - 1).astype(jnp.int32)
        notes = [head[rows : rows + 16, :].astype(jnp.float32)[0:1, 0:1] for head in (r_head, c_head)]
        centre = jnp.where(core == 0, *notes).astype(jnp.int32)
        excluded = zone[0:1, 0:1]
        free = (core - edge) * 4 * rows
        found = None
        for block in range(blocks):
            row_pos = block * BLOCK + lax.broadcasted_iota(jnp.int32, (BLOCK, rows), 0)
            col_pos = lax.broadcasted_iota(jnp.int32, (BLOCK, rows), 1)
            diff = col_pos - row_pos
            ahead = diff * (1 - 2 * edge)
            away = jnp.abs(ahead - centre)
            keep = (away <= quarter + free) & (rows + ahead + free >= excluded)
            total = pltpu.matmul_pop(totals[block]) + pltpu.matmul_pop(totals[blocks + block])
            score = jnp.where(keep, total, NEG)
            row_best = jnp.where(diff == 0, jnp.max(score, axis=1, keepdims=True), NEG)
            both = [jnp.max(value, axis=0, keepdims=True) for value in (score, row_best)]
            found = both if found is None else [jnp.maximum(*two) for two in zip(found, both)]
        best[0:1, :], best[1:2, :] = found

    in_unit(scoped, (BLOCK, rows), [unit for unit in range(UNITS) for _ in range(blocks)])


def tile_best(zone, r_head, r_tail, c_head, c_tail):
    rows, depth = r_tail.shape
    vmem = pl.BlockSpec(memory_space=pltpu.VMEM)
    return pl.pallas_call(
        tile_kernel,
        out_shape=jax.ShapeDtypeStruct((2, rows), jnp.float32),
        in_specs=[vmem, vmem, vmem, vmem, vmem],
        out_specs=vmem,
        scratch_shapes=[
            pltpu.VMEM((2, rows + M, depth), jnp.float32),
            pltpu.VMEM((2, rows, depth), jnp.float32),
            pltpu.VMEM((2, rows, depth), jnp.float32),
        ],
        compiler_params=pltpu.CompilerParams(vmem_limit_bytes=16 << 20),
        name="tile_best",
    )(zone, r_head, r_tail, c_head, c_tail)


def project_kernel(chunk, record, pca_map, partial_sum, samples, weights, arrived):
    copies = [pltpu.make_async_copy(pca_map, weights, arrived.at[0])]
    for first in range(0, record.shape[0], chunk):
        here = pl.ds(first, chunk)
        sem = arrived.at[1 + first // chunk]
        copies.append(pltpu.make_async_copy(record.at[here], samples.at[here], sem))
    for copy in copies:
        copy.start()
    copies[0].wait()
    for first, copy in zip(range(0, record.shape[0], chunk), copies[1:]):
        copy.wait()
        here = slice(first, first + chunk)
        partial_sum[here, :] = jnp.dot(
            samples[here, :], weights[...], preferred_element_type=jnp.float32
        )


def project(record, pca_map):
    rows, depth = record.shape[0], pca_map.shape[1]
    chunk = rows // CHUNKS
    hbm = pl.BlockSpec(memory_space=pltpu.HBM)
    return pl.pallas_call(
        functools.partial(project_kernel, chunk),
        out_shape=pltpu.VMEM((rows, depth), jnp.float32),
        in_specs=[hbm, hbm],
        out_specs=pl.BlockSpec(memory_space=pltpu.VMEM),
        scratch_shapes=[
            pltpu.VMEM(record.shape, record.dtype),
            pltpu.VMEM(pca_map.shape, pca_map.dtype),
            pltpu.SemaphoreType.DMA((1 + CHUNKS,)),
        ],
        compiler_params=pltpu.CompilerParams(vmem_limit_bytes=4 << 20),
        name="project",
    )(*(pltpu.with_memory_space_constraint(x, pltpu.HBM) for x in (record, pca_map)))


def fetched(value, sources):
    pairs = []
    for slab, both in enumerate(sources):
        pairs += [(2 * turn + core, 2 * slab + place) for place, (turn, core) in enumerate(both)]
    return lax.ppermute(value, ("tm", "chan"), pairs)


def swapped(value):
    return lax.ppermute(value, "chan", [(0, 1), (1, 0)])


def per_device(record, pca_map, offsets, exclusion):
    core = lax.axis_index("chan")
    cycle = lax.axis_size("tm")
    rows = record.shape[0]
    partial_value = project(record, pca_map)
    proj = (partial_value + swapped(partial_value)).astype(jnp.bfloat16)
    note = jnp.broadcast_to(offsets.astype(jnp.bfloat16)[:, None], (16, proj.shape[1]))
    noted = jnp.concatenate([proj, note], axis=0)
    half = cycle // 2
    turns = range(cycle)
    last = cycle - 1
    edge = (core == 1) & (lax.axis_index("tm") == last)
    first = [(((turn - 1) % cycle, 0), ((turn + half) % cycle, 1)) for turn in turns]
    second = [(((turn + 1) % cycle, 0), ((turn + half + 1) % cycle, 1)) for turn in turns]
    second[half - 1], second[last] = ((half, 1), (half, 0)), ((0, 0), (0, 1))
    third = [((turn, 1), ((turn + 1) % cycle, 0)) for turn in turns]
    for turn in range(1, last, 2):
        third[turn] = ((turn + 2, 1), third[turn][1])
    third[half - 1], third[last] = (third[half - 1][0], (0, 0)), ((half, 0), (1, 1))
    r_head, second, third = [fetched(noted, first), fetched(proj, second), fetched(proj, third)]
    r_head, second, third = lax.optimization_barrier((r_head, second, third))
    r_head = jnp.where(edge, jnp.concatenate([second, note], axis=0), r_head)
    turned = (core == 1) & (lax.axis_index("tm") % half == half - 1)
    r_tail = jnp.where(core == 0, proj, jnp.where(turned, third, second))
    c_tail = jnp.where((core == 1) & ~turned, third, second)
    zone = jnp.broadcast_to(exclusion[:, None], (8, proj.shape[1]))
    best = tile_best(zone, r_head, r_tail, noted, c_tail)
    beyond = [(turn - 1, 1) for turn in turns]
    beyond[0], beyond[half], beyond[last] = (0, 0), (last - 1, 1), (half - 1, 1)
    back = [((turn + 1, 0), beyond[turn]) for turn in turns[:-1]] + [((last, 1), beyond[last])]
    back = fetched(best[1], back)
    wanted = jnp.where(core == 0, lax.axis_index("tm") != last, edge)
    own = jnp.where(wanted, jnp.maximum(best[0], back), best[0])
    return jnp.maximum(own, swapped(own))


def solution(mesh):
    in_specs = (P(("groups", "tm"), "chan"), P("chan", None), P(("groups", "tm")), P("groups"))
    out_specs = P(("groups", "tm"))
    return jax.shard_map(
        per_device, mesh=mesh, in_specs=in_specs, out_specs=out_specs, check_vma=False
    )
```
